32 devices in a mesh: groups: 2 (over y), ctx: 4 (over z), head: 2 (over x), rep: 2 (over core).
Axes of the slice: x: 2, y: 2, z: 4, core: 2. Of those that a mesh axis runs over, the one named last changes fastest.
Arguments:
- hidden: bfloat16 [4096, 7168], P(('groups', 'ctx'), ('head', 'rep')), parts along dimension 0, may hold values from -6 to 6
- kv_down: bfloat16 [7168, 576], P(('head', 'rep')), may hold values from -0.0625 to 0.0625
- kv_gain: float32 [512], replicated, may hold values from 0.1 to 1.9
- queries: bfloat16 [16, 8, 192], P(('groups', 'rep'), ('ctx', 'head')), parts along dimension 0, may hold values from -512 to 512, as said below
- absorb_key: bfloat16 [8, 128, 512], P(('ctx', 'head')), may hold values from -0.5 to 0.5
- absorb_value: bfloat16 [8, 512, 128], P(('ctx', 'head')), may hold values from -0.75 to 0.75
- out_weight: bfloat16 [1024, 7168], P(('ctx', 'head')), may hold values from -0.1875 to 0.1875
- lengths: int32 [16], P(('groups', 'rep')), parts along dimension 0, may hold values from 512 to 2048
Outputs:
- layer_out: bfloat16 [16, 7168], P(('groups', 'rep'), ('ctx', 'head')), parts along dimension 0
The draws below stay inside these ranges and needn't reach their ends.
There are 2 independent parts, one for each index of `groups`. The reference program is written for one: setup_inputs(seed, part) draws one part's arguments, and reference() takes and returns one part's arrays. A program takes and returns all parts, laid end to end along the dimension named above; an argument that names none is the same for every part. Nothing has to cross between parts.
Inputs may be any that keep to these rules, and one draw needn't show every extreme that they name: Continuation b sees the first lengths[b] prompt positions. `queries`: entries are clipped normal values, of order one on most continuations; all query entries of one continuation may be scaled together by a common factor of at most 80.
All inputs are finite; a program needn't handle non-finite values.
Results may differ from the reference program's by a relative error of at most 0.025.
The reference program's roundings to bfloat16 on the way (of `kv_cache`, `qcat`, `attended` and `head_values`) count: a program that leaves them out, or rounds other values in their place, can miss the bound.
Values may be sent and summed in bfloat16 or wider, within the bound.
A program may use at most 64 MiB of HBM per device.

```python
import jax
import jax.numpy as jnp
from jax import lax

D = 7168
KV_RANK = 512
ROPE_DIM = 64
NOPE_DIM = 128
V_DIM = 128
HEADS = 8
TOKENS = 2048
CONTS = 8
LATENT = 576


def draw_queries(key, part):
    keys = jax.random.split(key, 1)
    base = jnp.clip(jax.random.normal(keys[0], (CONTS, HEADS, NOPE_DIM + ROPE_DIM), jnp.float32), -6.0, 6.0)
    return base.astype(jnp.bfloat16)


def place_ends(result, key, smallest, high):
    longest = result.shape.index(max(result.shape))
    spots = []
    for shift in (0, 1):
        where = [jax.random.randint(jax.random.fold_in(key, axis), (), 0, length) for axis, length in enumerate(result.shape)]
        where[longest] = (where[longest] + shift) % result.shape[longest]
        spots.append(tuple(where))
    return result.at[spots[0]].set(smallest).at[spots[1]].set(high)


def block_levels(rng, shape, shards, least, high):
    factor_of, own = 1.0, jax.random.fold_in(rng, 6)
    for axis_at, shards_of in shards:
        steps = jnp.exp(jax.random.uniform(jax.random.fold_in(own, axis_at), (shards_of,), jnp.float32, least / len(shards), high / len(shards)))
        factor_of = factor_of * jnp.repeat(steps, shape[axis_at] // shards_of).reshape([-1 if axis == axis_at else 1 for axis in range(len(shape))])
    return factor_of


def normal_values(key, dims, spread, most, pieces=(), held_as=jnp.bfloat16):
    array = spread * jax.random.normal(key, dims, jnp.float32)
    if pieces:
        array = array * block_levels(key, dims, pieces, -0.22, 0.18)
    return jnp.clip(array, -most, most).astype(held_as)


def setup_inputs(seed: int = 0, part: int = 0) -> dict:
    key_list = jax.random.split(jax.random.key(seed), 9)
    part_splits = jax.random.split(jax.random.fold_in(key_list[8], part), 9)
    return {
        "hidden": normal_values(part_splits[0], (TOKENS, D), 1.0, 6.0, ((0, 4), (1, 4))),
        "kv_down": normal_values(key_list[1], (D, LATENT), D ** -0.5, 0.0625, ((0, 4),)),
        "kv_gain": jnp.clip(1.0 + 0.18 * jax.random.normal(key_list[2], (KV_RANK,), jnp.float32), 0.1, 1.9),
        "queries": draw_queries(jax.random.fold_in(jax.random.fold_in(key_list[8], part), 71), part),
        "absorb_key": normal_values(key_list[4], (HEADS, NOPE_DIM, KV_RANK), NOPE_DIM ** -0.5, 0.5, ((0, 8),)),
        "absorb_value": normal_values(key_list[5], (HEADS, KV_RANK, V_DIM), (KV_RANK // 8) ** -0.5, 0.75, ((0, 8),)),
        "out_weight": normal_values(key_list[6], (HEADS * V_DIM, D), (HEADS * V_DIM) ** -0.5, 0.1875, ((0, 8),)),
        "lengths": place_ends(jax.random.randint(part_splits[7], (CONTS,), TOKENS // 4, TOKENS + 1), jax.random.fold_in(part_splits[7], 1), TOKENS // 4, TOKENS).astype(jnp.int32),
    }


def rotate(vectors, position):
    half_width = vectors.shape[-1] // 2
    frequency = 10000.0 ** (-jnp.arange(half_width, dtype=jnp.float32) / half_width)
    angles = position.astype(jnp.float32)[..., None] * frequency
    first_half = vectors[..., :half_width]
    second_half = vectors[..., half_width:]
    return jnp.concatenate([first_half * jnp.cos(angles) - second_half * jnp.sin(angles), first_half * jnp.sin(angles) + second_half * jnp.cos(angles)], -1)

def reference(hidden, kv_down, kv_gain, queries, absorb_key, absorb_value, out_weight, lengths):
    latent = jnp.dot(hidden, kv_down, preferred_element_type=jnp.float32)
    compressed = latent[:, :KV_RANK]
    normed = compressed * lax.rsqrt(lax.optimization_barrier(jnp.mean(compressed * compressed, -1, keepdims=True)) + 1e-06) * kv_gain
    positions = jnp.arange(TOKENS, dtype=jnp.int32)
    kv_cache = jnp.concatenate([normed, rotate(latent[:, KV_RANK:], positions)], -1).astype(jnp.bfloat16)
    q_latent = jnp.einsum('bhn,hnr->bhr', queries[..., :NOPE_DIM].astype(jnp.float32), absorb_key.astype(jnp.float32))
    q_rotary = rotate(queries[..., NOPE_DIM:].astype(jnp.float32), lengths[:, None])
    softmax_scale = (NOPE_DIM + ROPE_DIM) ** (-0.5)
    qcat = (jnp.concatenate([q_latent, q_rotary], -1) * softmax_scale).astype(jnp.bfloat16)

    def one_continuation(inputs):
        query_rows, length_one = inputs
        scores = jnp.dot(query_rows, kv_cache.T, preferred_element_type=jnp.float32)
        visible = (positions < length_one)[None, :]
        masked = jnp.where(visible, scores, -1e+30)
        row_max = lax.optimization_barrier(jnp.max(masked, -1, keepdims=True))
        weights = jnp.where(visible, jnp.exp(masked - row_max), 0.0)
        denominator = lax.optimization_barrier(jnp.sum(weights, -1, keepdims=True))
        context = jnp.dot(weights.astype(jnp.bfloat16), kv_cache[:, :KV_RANK], preferred_element_type=jnp.float32)
        return (context / denominator).astype(jnp.bfloat16)
    attended = lax.map(one_continuation, (qcat, lengths))
    head_values = jnp.einsum('bhr,hrv->bhv', attended.astype(jnp.float32), absorb_value.astype(jnp.float32)).astype(jnp.bfloat16)
    flat_values = head_values.reshape(CONTS, HEADS * V_DIM)
    return jnp.dot(flat_values, out_weight, preferred_element_type=jnp.float32).astype(jnp.bfloat16)
```

```python
import functools

import jax
import jax.numpy as jnp
import numpy as np
from jax import lax
from jax.experimental import pallas as pl
from jax.experimental.pallas import tpu as pltpu
from jax.sharding import PartitionSpec as P

MESH = pl.DeviceIdType.MESH
LANES = 128


def rotate(vectors, position):
    half_width = vectors.shape[-1] // 2
    frequency = 10000.0 ** (-jnp.arange(half_width, dtype=jnp.float32) / half_width)
    angles = position.astype(jnp.float32)[..., None] * frequency
    first_half = vectors[..., :half_width]
    second_half = vectors[..., half_width:]
    return jnp.concatenate(
        [
            first_half * jnp.cos(angles) - second_half * jnp.sin(angles),
            first_half * jnp.sin(angles) + second_half * jnp.cos(angles),
        ],
        -1,
    )


def finish_rows(latent, kv_gain, first_row):
    rank_width = kv_gain.shape[0]
    compressed = latent[:, :rank_width]
    normed = (
        compressed
        * lax.rsqrt(jnp.mean(compressed * compressed, -1, keepdims=True) + 1e-06)
        * kv_gain
    )
    positions = first_row + jnp.arange(latent.shape[0], dtype=jnp.int32)
    return jnp.concatenate([normed, rotate(latent[:, rank_width:], positions)], -1).astype(
        jnp.bfloat16
    )


def shards(hidden, kv_down, kv_gain, queries, absorb_key, absorb_value, out_weight, lengths):
    tok_rows = hidden.shape[0]
    rank_width = kv_gain.shape[0]
    nope_width = absorb_key.shape[1]
    heads_dev = queries.shape[1]
    first_row = lax.axis_index("ctx") * tok_rows
    partial_value = jnp.dot(hidden, kv_down, preferred_element_type=jnp.float32)
    whole_latent = lax.psum(partial_value, ("head", "rep"))
    kv_cache = finish_rows(whole_latent, kv_gain, first_row)
    q_latent = jnp.einsum(
        "bhn,hnr->bhr", queries[..., :nope_width], absorb_key, preferred_element_type=jnp.float32
    )
    q_rotary = rotate(queries[..., nope_width:].astype(jnp.float32), lengths[:, None])
    softmax_scale = queries.shape[2] ** (-0.5)
    qcat = (jnp.concatenate([q_latent, q_rotary], -1) * softmax_scale).astype(jnp.bfloat16)
    gathered = lax.all_gather(qcat, "ctx", axis=1, tiled=True)
    cont_rows = gathered.shape[0]
    head_rows = gathered.shape[1]
    flat_queries = gathered.reshape(cont_rows * head_rows, gathered.shape[2])
    scores = jnp.dot(flat_queries, kv_cache.T, preferred_element_type=jnp.float32).reshape(
        cont_rows, head_rows, tok_rows
    )
    positions = first_row + jnp.arange(tok_rows, dtype=jnp.int32)
    visible = positions[None, None, :] < lengths[:, None, None]
    masked = jnp.where(visible, scores, -1e30)
    row_max = jnp.max(masked, -1)
    weights = jnp.where(visible, jnp.exp(masked - row_max[..., None]), 0.0)
    denominator = jnp.sum(weights, -1)
    flat_weights = weights.astype(jnp.bfloat16).reshape(cont_rows * head_rows, tok_rows)
    context = jnp.dot(
        flat_weights, kv_cache[:, :rank_width], preferred_element_type=jnp.float32
    ).reshape(cont_rows, head_rows, rank_width)
    top_peak = lax.pmax(row_max, "ctx")
    factor = jnp.exp(row_max - top_peak)
    total_own, context_own = (
        lax.psum_scatter(
            (denominator * factor).astype(jnp.bfloat16), "ctx", scatter_dimension=1, tiled=True
        ).astype(jnp.float32),
        lax.psum_scatter(
            (context * factor[..., None]).astype(jnp.bfloat16),
            "ctx",
            scatter_dimension=1,
            tiled=True,
        ).astype(jnp.float32),
    )
    attended = (context_own / total_own[..., None]).astype(jnp.bfloat16)
    head_values = jnp.einsum(
        "bhr,hrv->bhv", attended, absorb_value, preferred_element_type=jnp.float32
    ).astype(jnp.bfloat16)
    flat_values = head_values.reshape(cont_rows, heads_dev * head_values.shape[2])
    out_partial = jnp.dot(flat_values, out_weight, preferred_element_type=jnp.float32)
    return lax.psum_scatter(out_partial, ("ctx", "head"), scatter_dimension=1, tiled=True).astype(
        jnp.bfloat16
    )


def rotary_table(positions, rope_width):
    half_width = rope_width // 2
    frequency = (
        10000.0 ** (-np.arange(half_width, dtype=np.float32) / np.float32(half_width)).astype(np.float64)
    ).astype(np.float32)
    angles = (np.arange(positions, dtype=np.float32)[:, None] * frequency).astype(np.float64)
    cosine, sine = np.cos(angles), np.sin(angles)
    return np.concatenate([cosine, cosine, -sine, sine], -1).astype(np.float32)


def swap_halves(x):
    half = x.shape[-1] // 2
    return jnp.concatenate([x[:, half:], x[:, :half]], -1)


def split3(x):
    first = x.astype(jnp.bfloat16).astype(jnp.float32)
    second = (x - first).astype(jnp.bfloat16).astype(jnp.float32)
    return first, second, x - first - second


def lane_tile(columns, rows):
    lane = lax.broadcasted_iota(jnp.int32, (rows, LANES), 1)
    tile = jnp.zeros((rows, LANES), jnp.float32)
    for i, column in enumerate(columns):
        tile = jnp.where(lane == i, column, tile)
    return tile


def fused_kernel(
    n_ctx, n_head, n_rep,
    hidden, kv_down, gain, queries, absorb_key, absorb_value, out_weight, lengths, table,
    out,
    h_buf, kd_buf, gain_buf, q_buf, ak_buf, av_buf, ow_buf, tab_buf,
    pc, pr, rc, rr, sc, sr, xc, xr,
    q_all, o_send, o_recv, y_send, y_recv,
    load_sem, rep_send, rep_recv, head_send, head_recv,
    q_ssem, q_rsem, o_ssem, o_rsem, y_ssem, y_rsem,
):
    g, c = lax.axis_index("groups"), lax.axis_index("ctx")
    h, r = lax.axis_index("head"), lax.axis_index("rep")
    n_all, n_out = n_ctx * n_head * n_rep, n_ctx * n_head
    me, me_out = (c * n_head + h) * n_rep + r, c * n_head + h
    tok_rows = hidden.shape[0]
    rows = tok_rows // (n_head * n_rep)
    rank = gain_buf.shape[1]
    conts = queries.shape[0]
    nope = absorb_key.shape[1]
    rope = queries.shape[2] - nope
    width = q_all.shape[2]
    out_cols = y_send.shape[2]
    f32, bf16 = jnp.float32, jnp.bfloat16

    def peer(index):
        return (g, index // (n_head * n_rep), (index // n_rep) % n_head, index % n_rep)

    barrier = pltpu.get_barrier_semaphore()
    for k in range(1, n_all):
        pl.semaphore_signal(
            barrier, inc=1, device_id=peer((me + k) % n_all), device_id_type=MESH
        )

    loads = {}

    def load(name, source, target):
        loads[name] = pltpu.make_async_copy(source, target, load_sem.at[len(loads)])
        loads[name].start()

    head_order = list(range(1, n_head)) + [0]

    def load_hidden(k):
        for k2 in range(n_rep):
            block = ((h + k) % n_head) * n_rep + (r + k2) % n_rep
            load(
                ("hidden", k, k2),
                hidden.at[pl.ds(pl.multiple_of(block * rows, 8), rows), :],
                h_buf.at[k, pl.ds(k2 * rows, rows), :],
            )

    load_hidden(head_order[0])
    load("kd", kv_down, kd_buf)
    load("q", queries, q_buf)
    load("ak", absorb_key, ak_buf)
    load("table", table, tab_buf)
    for k in head_order[1:]:
        load_hidden(k)
    load("gain", gain, gain_buf)
    load("av", absorb_value, av_buf)
    for k in range(n_out):
        column = pl.multiple_of(((me_out + k) % n_out) * out_cols, LANES)
        load(("ow", k), out_weight.at[:, pl.ds(column, out_cols)], ow_buf.at[k])

    def remote(source, target, send_sem, recv_sem, device):
        return pltpu.make_async_remote_copy(
            src_ref=source, dst_ref=target, send_sem=send_sem, recv_sem=recv_sem,
            device_id=device, device_id_type=MESH,
        )

    copies = []

    def project(k):
        for k2 in range(n_rep):
            loads["hidden", k, k2].wait()
        partial = jnp.dot(h_buf[k], kd_buf[...], preferred_element_type=f32)
        for k2 in range(n_rep):
            block = partial[k2 * rows : (k2 + 1) * rows]
            pc[k, k2] = block[:, :rank]
            pr[k, k2] = jnp.concatenate([block[: rows // 2, rank:], block[rows // 2 :, rank:]], -1)

    def exchange_rep(k):
        started = []
        for k2 in range(1, n_rep):
            to = (g, c, h, (r + k2) % n_rep)
            slot = (k * n_rep + k2) * 2
            for j, (source, target) in enumerate(((pc, rc), (pr, rr))):
                copy = remote(
                    source.at[k, k2], target.at[k, k2],
                    rep_send.at[slot + j], rep_recv.at[slot + j], to,
                )
                copy.start()
                started.append(copy)
        copies.extend(started)
        return started

    def sum_rep(k, started):
        for copy in started:
            copy.wait_recv()
        total_c, total_r = pc[k, 0], pr[k, 0]
        for k2 in range(1, n_rep):
            total_c, total_r = total_c + rc[k, k2], total_r + rr[k, k2]
        sc[k], sr[k] = total_c, total_r

    def exchange_head(k):
        to = (g, c, (h + k) % n_head, r)
        started = []
        for j, (source, target) in enumerate(((sc, xc), (sr, xr))):
            copy = remote(
                source.at[k], target.at[k], head_send.at[k * 2 + j], head_recv.at[k * 2 + j], to
            )
            copy.start()
            started.append(copy)
        copies.extend(started)
        return started

    loads["kd"].wait()
    first = head_order[0]
    project(first)
    pl.semaphore_wait(barrier, n_all - 1)
    in_flight = {first: exchange_rep(first)}

    for name in ("q", "ak", "table"):
        loads[name].wait()
    own_q = q_buf[:, 0, :]
    q_latent = jnp.dot(own_q[:, :nope], ak_buf[0], preferred_element_type=f32)
    q_rotary = own_q[:, nope:].astype(f32)
    angles = jnp.concatenate([tab_buf[pl.ds(lengths[b], 1), :] for b in range(conts)], 0)
    q_rotary = q_rotary * angles[:, :rope] + swap_halves(q_rotary) * angles[:, rope:]
    scale = queries.shape[2] ** (-0.5)
    row = lax.broadcasted_iota(jnp.int32, (conts, LANES), 0)
    length_rows = jnp.zeros((conts, LANES), jnp.int32)
    for b in range(conts):
        length_rows = jnp.where(row == b, lengths[b], length_rows)
    high = length_rows // 64
    lane = lax.broadcasted_iota(jnp.int32, (conts, LANES), 1)
    extra = jnp.where(lane == 0, high, length_rows - high * 64).astype(f32)[:, : width - rank - rope]
    qcat = jnp.concatenate([q_latent * scale, q_rotary * scale, extra], -1)
    q_all[0] = qcat.astype(bf16)
    q_copies = []
    for k in range(1, n_all):
        copy = remote(
            q_all.at[0], q_all.at[k], q_ssem.at[k], q_rsem.at[k], peer((me + k) % n_all)
        )
        copy.start()
        q_copies.append(copy)
    copies.extend(q_copies)

    sent = []
    if n_head > 1:
        sum_rep(first, in_flight[first])
        sent += exchange_head(first)
        for k in head_order[1:]:
            project(k)
            started = exchange_rep(k)
            sum_rep(k, started)
            if k:
                sent += exchange_head(k)
    else:
        sum_rep(first, in_flight[first])

    for copy in q_copies:
        copy.wait_recv()
    q_rows = jnp.concatenate([q_all[k].astype(f32) for k in range(n_all)], 0)
    q_lengths = q_rows[:, rank + rope : rank + rope + 1] * 64.0 + q_rows[
        :, rank + rope + 1 : rank + rope + 2
    ]
    loads["gain"].wait()
    base = c * tok_rows + (h * n_rep + r) * rows
    token_table = tab_buf[pl.ds(pl.multiple_of(base, 8), rows), :]

    for copy in sent:
        copy.wait_recv()
    latent_c, latent_r = sc[0], sr[0]
    for k in range(1, n_head):
        latent_c, latent_r = latent_c + xc[k], latent_r + xr[k]
    latent_r = jnp.concatenate([latent_r[:, :rope], latent_r[:, rope:]], 0)
    normed = (
        latent_c
        * lax.rsqrt(jnp.mean(latent_c * latent_c, -1, keepdims=True) + 1e-06)
        * gain_buf[...]
    )
    rotary = latent_r * token_table[:, :rope] + swap_halves(latent_r) * token_table[:, rope:]
    kv_c = normed.astype(bf16)
    kv = jnp.concatenate(
        [normed, rotary, jnp.zeros((rows, width - rank - rope), f32)], -1
    ).astype(bf16)
    scores = lax.dot_general(
        q_rows.astype(bf16), kv, (((1,), (1,)), ((), ())), preferred_element_type=f32
    )
    n_q = n_all * conts
    positions = (base + lax.broadcasted_iota(jnp.int32, (n_q, rows), 1)).astype(f32)
    visible = positions < q_lengths
    masked = jnp.where(visible, scores, -1e30)
    row_max = jnp.max(masked, -1, keepdims=True)
    weights = jnp.where(visible, jnp.exp(masked - row_max), 0.0)
    total = jnp.sum(weights, -1, keepdims=True)
    context = jnp.dot(weights.astype(bf16), kv_c, preferred_element_type=f32)
    stats = lane_tile(split3(row_max) + split3(total), n_q)
    for k in range(n_all):
        block = slice(k * conts, (k + 1) * conts)
        target = o_recv if k == 0 else o_send
        target[k, :, :rank] = context[block].astype(bf16)
        target[k, :, rank:] = stats[block].astype(bf16)
    o_copies = []
    for k in range(1, n_all):
        copy = remote(
            o_send.at[k], o_recv.at[k], o_ssem.at[k], o_rsem.at[k],
            peer((me + n_all - k) % n_all),
        )
        copy.start()
        o_copies.append(copy)
    copies.extend(o_copies)
    loads["av"].wait()
    for k in range(n_out):
        loads["ow", k].wait()
    for copy in o_copies:
        copy.wait_recv()

    parts, maxima, totals = [], [], []
    for k in range(n_all):
        part = o_recv[k].astype(f32)
        parts.append(part[:, :rank])
        s = part[:, rank:]
        maxima.append(s[:, 0:1] + s[:, 1:2] + s[:, 2:3])
        totals.append(s[:, 3:4] + s[:, 4:5] + s[:, 5:6])
    top = functools.reduce(jnp.maximum, maxima)
    factors = [jnp.exp(m - top) for m in maxima]
    total_own = sum(f * t for f, t in zip(factors, totals))
    context_own = sum(f * p for f, p in zip(factors, parts))
    attended = (context_own / total_own).astype(bf16)
    head_values = jnp.dot(attended, av_buf[0], preferred_element_type=f32).astype(bf16)
    y_copies = []
    for k in range(1, n_out):
        y_send[k] = jnp.dot(head_values, ow_buf[k], preferred_element_type=f32).astype(y_send.dtype)
        to = (me_out + k) % n_out
        copy = remote(
            y_send.at[k], y_recv.at[k], y_ssem.at[k], y_rsem.at[k],
            (g, to // n_head, to % n_head, r),
        )
        copy.start()
        y_copies.append(copy)
    copies.extend(y_copies)
    result = jnp.dot(head_values, ow_buf[0], preferred_element_type=f32)
    for k in range(1, n_out):
        y_copies[k - 1].wait_recv()
        result = result + y_recv[k].astype(f32)
    out[...] = result.astype(out.dtype)
    for copy in copies:
        copy.wait_send()


def fused(mesh, hidden, kv_down, kv_gain, queries, absorb_key, absorb_value, out_weight, lengths):
    n_ctx, n_head, n_rep = (mesh.shape[a] for a in ("ctx", "head", "rep"))
    n_all, n_out = n_ctx * n_head * n_rep, n_ctx * n_head
    tok_rows, width_dev = hidden.shape
    rows = tok_rows // (n_head * n_rep)
    rank = kv_gain.shape[0]
    latent_width = kv_down.shape[1]
    rope = latent_width - rank
    conts = queries.shape[0]
    padded = rank + LANES
    out_cols = out_weight.shape[1] // n_out
    positions = -(-(n_ctx * tok_rows + 1) // 8) * 8
    table = jnp.asarray(rotary_table(positions, rope))
    f32, bf16 = jnp.float32, jnp.bfloat16
    dma = lambda *shape: pltpu.SemaphoreType.DMA(shape)
    any_space = pl.BlockSpec(memory_space=pl.ANY)
    vmem = pltpu.VMEM
    n_loads = n_head * n_rep + 6 + n_out
    pair_c, pair_r = (n_head, n_rep, rows, rank), (n_head, n_rep, rows // 2, 2 * rope)
    return pl.pallas_call(
        functools.partial(fused_kernel, n_ctx, n_head, n_rep),
        out_shape=jax.ShapeDtypeStruct((conts, out_cols), bf16),
        in_specs=[any_space] * 7 + [pl.BlockSpec(memory_space=pltpu.SMEM), any_space],
        out_specs=pl.BlockSpec(memory_space=vmem),
        scratch_shapes=[
            vmem((n_head, n_rep * rows, width_dev), bf16),
            vmem(kv_down.shape, bf16),
            vmem((1, rank), f32),
            vmem(queries.shape, bf16),
            vmem(absorb_key.shape, bf16),
            vmem(absorb_value.shape, bf16),
            vmem((n_out, out_weight.shape[0], out_cols), bf16),
            vmem(table.shape, f32),
            vmem(pair_c, f32), vmem(pair_r, f32),
            vmem(pair_c, f32), vmem(pair_r, f32),
            vmem(pair_c[:1] + pair_c[2:], f32), vmem(pair_r[:1] + pair_r[2:], f32),
            vmem(pair_c[:1] + pair_c[2:], f32), vmem(pair_r[:1] + pair_r[2:], f32),
            vmem((n_all, conts, padded), bf16),
            vmem((n_all, conts, padded), bf16),
            vmem((n_all, conts, padded), bf16),
            vmem((n_out, conts, out_cols), bf16),
            vmem((n_out, conts, out_cols), bf16),
            dma(n_loads),
            dma(n_head * n_rep * 2), dma(n_head * n_rep * 2),
            dma(n_head * 2), dma(n_head * 2),
            dma(n_all), dma(n_all), dma(n_all), dma(n_all), dma(n_out), dma(n_out),
        ],
        compiler_params=pltpu.CompilerParams(collective_id=0, has_side_effects=True),
    )(
        hidden, kv_down, kv_gain.reshape(1, rank), queries, absorb_key, absorb_value,
        out_weight, lengths, table,
    )


def body(mesh, *arrays):
    hidden, kv_down, kv_gain, queries, absorb_key, _, out_weight, _ = arrays
    n_ctx, n_head, n_rep = (mesh.shape[a] for a in ("ctx", "head", "rep"))
    rope = kv_down.shape[1] - kv_gain.shape[0]
    whole_tiles = (
        queries.shape[1] == 1
        and 2 * rope == LANES
        and queries.shape[2] - absorb_key.shape[1] == rope
        and kv_gain.shape[0] % LANES == 0
        and hidden.shape[0] % (n_head * n_rep * 32) == 0
        and out_weight.shape[1] % (n_ctx * n_head * LANES) == 0
    )
    return fused(mesh, *arrays) if whole_tiles else shards(*arrays)


def solution(mesh):
    return jax.shard_map(
        functools.partial(body, mesh),
        mesh=mesh,
        in_specs=(
            P(("groups", "ctx"), ("head", "rep")),
            P(("head", "rep"), None),
            P(),
            P(("groups", "rep"), ("ctx", "head"), None),
            P(("ctx", "head"), None, None),
            P(("ctx", "head"), None, None),
            P(("ctx", "head"), None),
            P(("groups", "rep")),
        ),
        out_specs=P(("groups", "rep"), ("ctx", "head")),
        check_vma=False,
    )
```

```python
import functools

import jax
import jax.numpy as jnp
import numpy as np
from jax import lax
from jax.experimental import pallas as pl
from jax.experimental.pallas import tpu as pltpu
from jax.sharding import PartitionSpec as P

MESH = pl.DeviceIdType.MESH
LANES = 128


def rotate(vectors, position):
    half_width = vectors.shape[-1] // 2
    frequency = 10000.0 ** (-jnp.arange(half_width, dtype=jnp.float32) / half_width)
    angles = position.astype(jnp.float32)[..., None] * frequency
    first_half = vectors[..., :half_width]
    second_half = vectors[..., half_width:]
    return jnp.concatenate(
        [
            first_half * jnp.cos(angles) - second_half * jnp.sin(angles),
            first_half * jnp.sin(angles) + second_half * jnp.cos(angles),
        ],
        -1,
    )


def finish_rows(latent, kv_gain, first_row):
    rank_width = kv_gain.shape[0]
    compressed = latent[:, :rank_width]
    normed = (
        compressed
        * lax.rsqrt(jnp.mean(compressed * compressed, -1, keepdims=True) + 1e-06)
        * kv_gain
    )
    positions = first_row + jnp.arange(latent.shape[0], dtype=jnp.int32)
    return jnp.concatenate([normed, rotate(latent[:, rank_width:], positions)], -1).astype(
        jnp.bfloat16
    )


def shards(hidden, kv_down, kv_gain, queries, absorb_key, absorb_value, out_weight, lengths):
    tok_rows = hidden.shape[0]
    rank_width = kv_gain.shape[0]
    nope_width = absorb_key.shape[1]
    heads_dev = queries.shape[1]
    first_row = lax.axis_index("ctx") * tok_rows
    partial_value = jnp.dot(hidden, kv_down, preferred_element_type=jnp.float32)
    whole_latent = lax.psum(partial_value, ("head", "rep"))
    kv_cache = finish_rows(whole_latent, kv_gain, first_row)
    q_latent = jnp.einsum(
        "bhn,hnr->bhr", queries[..., :nope_width], absorb_key, preferred_element_type=jnp.float32
    )
    q_rotary = rotate(queries[..., nope_width:].astype(jnp.float32), lengths[:, None])
    softmax_scale = queries.shape[2] ** (-0.5)
    qcat = (jnp.concatenate([q_latent, q_rotary], -1) * softmax_scale).astype(jnp.bfloat16)
    gathered = lax.all_gather(qcat, "ctx", axis=1, tiled=True)
    cont_rows = gathered.shape[0]
    head_rows = gathered.shape[1]
    flat_queries = gathered.reshape(cont_rows * head_rows, gathered.shape[2])
    scores = jnp.dot(flat_queries, kv_cache.T, preferred_element_type=jnp.float32).reshape(
        cont_rows, head_rows, tok_rows
    )
    positions = first_row + jnp.arange(tok_rows, dtype=jnp.int32)
    visible = positions[None, None, :] < lengths[:, None, None]
    masked = jnp.where(visible, scores, -1e30)
    row_max = jnp.max(masked, -1)
    weights = jnp.where(visible, jnp.exp(masked - row_max[..., None]), 0.0)
    denominator = jnp.sum(weights, -1)
    flat_weights = weights.astype(jnp.bfloat16).reshape(cont_rows * head_rows, tok_rows)
    context = jnp.dot(
        flat_weights, kv_cache[:, :rank_width], preferred_element_type=jnp.float32
    ).reshape(cont_rows, head_rows, rank_width)
    top_peak = lax.pmax(row_max, "ctx")
    factor = jnp.exp(row_max - top_peak)
    total_own, context_own = (
        lax.psum_scatter(
            (denominator * factor).astype(jnp.bfloat16), "ctx", scatter_dimension=1, tiled=True
        ).astype(jnp.float32),
        lax.psum_scatter(
            (context * factor[..., None]).astype(jnp.bfloat16),
            "ctx",
            scatter_dimension=1,
            tiled=True,
        ).astype(jnp.float32),
    )
    attended = (context_own / total_own[..., None]).astype(jnp.bfloat16)
    head_values = jnp.einsum(
        "bhr,hrv->bhv", attended, absorb_value, preferred_element_type=jnp.float32
    ).astype(jnp.bfloat16)
    flat_values = head_values.reshape(cont_rows, heads_dev * head_values.shape[2])
    out_partial = jnp.dot(flat_values, out_weight, preferred_element_type=jnp.float32)
    return lax.psum_scatter(out_partial, ("ctx", "head"), scatter_dimension=1, tiled=True).astype(
        jnp.bfloat16
    )


def rotary_table(positions, rope_width):
    half_width = rope_width // 2
    frequency = (
        10000.0 ** (-np.arange(half_width, dtype=np.float32) / np.float32(half_width)).astype(np.float64)
    ).astype(np.float32)
    angles = (np.arange(positions, dtype=np.float32)[:, None] * frequency).astype(np.float64)
    cosine, sine = np.cos(angles), np.sin(angles)
    return np.concatenate([cosine, cosine, -sine, sine], -1).astype(np.float32)


def swap_halves(x):
    half = x.shape[-1] // 2
    return jnp.concatenate([x[:, half:], x[:, :half]], -1)


def split3(x):
    first = x.astype(jnp.bfloat16).astype(jnp.float32)
    second = (x - first).astype(jnp.bfloat16).astype(jnp.float32)
    return first, second, x - first - second


def lane_tile(columns, rows):
    lane = lax.broadcasted_iota(jnp.int32, (rows, LANES), 1)
    tile = jnp.zeros((rows, LANES), jnp.float32)
    for i, column in enumerate(columns):
        tile = jnp.where(lane == i, column, tile)
    return tile


def fused_kernel(
    n_ctx, n_head, n_rep,
    hidden, kv_down, gain, queries, absorb_key, absorb_value, out_weight, lengths, table,
    out,
    h_buf, kd_buf, gain_buf, q_buf, ak_buf, av_buf, ow_buf, tab_buf,
    pc, pr, rc, rr, sc, sr, xc, xr,
    q_all, o_send, o_recv, y_send, y_recv,
    load_sem, rep_send, rep_recv, head_send, head_recv,
    q_ssem, q_rsem, o_ssem, o_rsem, y_ssem, y_rsem,
):
    g, c = lax.axis_index("groups"), lax.axis_index("ctx")
    h, r = lax.axis_index("head"), lax.axis_index("rep")
    n_all, n_out = n_ctx * n_head * n_rep, n_ctx * n_head
    me, me_out = (c * n_head + h) * n_rep + r, c * n_head + h
    tok_rows = hidden.shape[0]
    rows = tok_rows // (n_head * n_rep)
    rank = gain_buf.shape[1]
    conts = queries.shape[1]
    nope = absorb_key.shape[1]
    rope = queries.shape[2] - nope
    width = q_all.shape[2]
    out_cols = y_send.shape[2]
    f32, bf16 = jnp.float32, jnp.bfloat16

    def peer(index):
        return (g, index // (n_head * n_rep), (index // n_rep) % n_head, index % n_rep)

    barrier = pltpu.get_barrier_semaphore()
    for k in range(1, n_all):
        pl.semaphore_signal(
            barrier, inc=1, device_id=peer((me + k) % n_all), device_id_type=MESH
        )

    loads = {}

    def load(name, source, target):
        loads[name] = pltpu.make_async_copy(source, target, load_sem.at[len(loads)])
        loads[name].start()

    head_order = list(range(1, n_head)) + [0]

    def load_hidden(k):
        for k2 in range(n_rep):
            block = ((h + k) % n_head) * n_rep + (r + k2) % n_rep
            load(
                ("hidden", k, k2),
                hidden.at[pl.ds(pl.multiple_of(block * rows, 8), rows), :],
                h_buf.at[k, pl.ds(k2 * rows, rows), :],
            )

    load_hidden(head_order[0])
    load("kd", kv_down, kd_buf)
    load("q", queries, q_buf)
    load("ak", absorb_key, ak_buf)
    load("table", table, tab_buf)
    for k in head_order[1:]:
        load_hidden(k)
    load("gain", gain, gain_buf)
    load("av", absorb_value, av_buf)
    for k in range(n_out):
        column = pl.multiple_of(((me_out + k) % n_out) * out_cols, LANES)
        load(("ow", k), out_weight.at[:, pl.ds(column, out_cols)], ow_buf.at[k])

    def remote(source, target, send_sem, recv_sem, device):
        return pltpu.make_async_remote_copy(
            src_ref=source, dst_ref=target, send_sem=send_sem, recv_sem=recv_sem,
            device_id=device, device_id_type=MESH,
        )

    copies = []

    def project(k):
        for k2 in range(n_rep):
            loads["hidden", k, k2].wait()
        partial = lax.dot_general(
            h_buf[k], kd_buf[...], (((1,), (1,)), ((), ())), preferred_element_type=f32
        )
        for k2 in range(n_rep):
            block = partial[k2 * rows : (k2 + 1) * rows]
            pc[k, k2] = block[:, :rank]
            pr[k, k2] = jnp.concatenate([block[: rows // 2, rank:], block[rows // 2 :, rank:]], -1)

    def exchange_rep(k):
        started = []
        for k2 in range(1, n_rep):
            to = (g, c, h, (r + k2) % n_rep)
            slot = (k * n_rep + k2) * 2
            for j, (source, target) in enumerate(((pc, rc), (pr, rr))):
                copy = remote(
                    source.at[k, k2], target.at[k, k2],
                    rep_send.at[slot + j], rep_recv.at[slot + j], to,
                )
                copy.start()
                started.append(copy)
        copies.extend(started)
        return started

    def sum_rep(k, started):
        for copy in started:
            copy.wait_recv()
        total_c, total_r = pc[k, 0], pr[k, 0]
        for k2 in range(1, n_rep):
            total_c, total_r = total_c + rc[k, k2], total_r + rr[k, k2]
        sc[k], sr[k] = total_c, total_r

    def exchange_head(k):
        to = (g, c, (h + k) % n_head, r)
        started = []
        for j, (source, target) in enumerate(((sc, xc), (sr, xr))):
            copy = remote(
                source.at[k], target.at[k], head_send.at[k * 2 + j], head_recv.at[k * 2 + j], to
            )
            copy.start()
            started.append(copy)
        copies.extend(started)
        return started

    loads["kd"].wait()
    first = head_order[0]
    project(first)
    pl.semaphore_wait(barrier, n_all - 1)
    in_flight = {first: exchange_rep(first)}

    for name in ("q", "ak", "table"):
        loads[name].wait()
    own_q = q_buf[0]
    q_latent = jnp.dot(own_q[:, :nope], ak_buf[0], preferred_element_type=f32)
    q_rotary = own_q[:, nope:].astype(f32)
    angles = jnp.concatenate([tab_buf[pl.ds(lengths[b], 1), :] for b in range(conts)], 0)
    q_rotary = q_rotary * angles[:, :rope] + swap_halves(q_rotary) * angles[:, rope:]
    scale = queries.shape[2] ** (-0.5)
    row = lax.broadcasted_iota(jnp.int32, (conts, LANES), 0)
    length_rows = jnp.zeros((conts, LANES), jnp.int32)
    for b in range(conts):
        length_rows = jnp.where(row == b, lengths[b], length_rows)
    high = length_rows // 64
    lane = lax.broadcasted_iota(jnp.int32, (conts, LANES), 1)
    extra = jnp.where(lane == 0, high, length_rows - high * 64).astype(f32)[:, : width - rank - rope]
    qcat = jnp.concatenate([q_latent * scale, q_rotary * scale, extra], -1)
    q_all[0] = qcat.astype(bf16)
    q_copies = []
    for k in range(1, n_all):
        copy = remote(
            q_all.at[0], q_all.at[k], q_ssem.at[k], q_rsem.at[k], peer((me + k) % n_all)
        )
        copy.start()
        q_copies.append(copy)
    copies.extend(q_copies)

    sent = []
    if n_head > 1:
        sum_rep(first, in_flight[first])
        sent += exchange_head(first)
        for k in head_order[1:]:
            project(k)
            started = exchange_rep(k)
            sum_rep(k, started)
            if k:
                sent += exchange_head(k)
    else:
        sum_rep(first, in_flight[first])

    for copy in q_copies:
        copy.wait_recv()
    q_rows = jnp.concatenate([q_all[k].astype(f32) for k in range(n_all)], 0)
    q_lengths = q_rows[:, rank + rope : rank + rope + 1] * 64.0 + q_rows[
        :, rank + rope + 1 : rank + rope + 2
    ]
    loads["gain"].wait()
    base = c * tok_rows + (h * n_rep + r) * rows
    token_table = tab_buf[pl.ds(pl.multiple_of(base, 8), rows), :]

    for copy in sent:
        copy.wait_recv()
    latent_c, latent_r = sc[0], sr[0]
    for k in range(1, n_head):
        latent_c, latent_r = latent_c + xc[k], latent_r + xr[k]
    latent_r = jnp.concatenate([latent_r[:, :rope], latent_r[:, rope:]], 0)
    normed = (
        latent_c
        * lax.rsqrt(jnp.mean(latent_c * latent_c, -1, keepdims=True) + 1e-06)
        * gain_buf[...]
    )
    rotary = latent_r * token_table[:, :rope] + swap_halves(latent_r) * token_table[:, rope:]
    kv_c = normed.astype(bf16)
    kv = jnp.concatenate(
        [normed, rotary, jnp.zeros((rows, width - rank - rope), f32)], -1
    ).astype(bf16)
    scores = lax.dot_general(
        q_rows.astype(bf16), kv, (((1,), (1,)), ((), ())), preferred_element_type=f32
    )
    n_q = n_all * conts
    positions = (base + lax.broadcasted_iota(jnp.int32, (n_q, rows), 1)).astype(f32)
    visible = positions < q_lengths
    masked = jnp.where(visible, scores, -1e30)
    row_max = jnp.max(masked, -1, keepdims=True)
    weights = jnp.where(visible, jnp.exp(masked - row_max), 0.0)
    total = jnp.sum(weights, -1, keepdims=True)
    context = jnp.dot(weights.astype(bf16), kv_c, preferred_element_type=f32)
    stats = lane_tile(split3(row_max) + split3(total), n_q)
    for k in range(n_all):
        block = slice(k * conts, (k + 1) * conts)
        target = o_recv if k == 0 else o_send
        target[k, :, :rank] = context[block].astype(bf16)
        target[k, :, rank:] = stats[block].astype(bf16)
    o_copies = []
    for k in range(1, n_all):
        copy = remote(
            o_send.at[k], o_recv.at[k], o_ssem.at[k], o_rsem.at[k],
            peer((me + n_all - k) % n_all),
        )
        copy.start()
        o_copies.append(copy)
    copies.extend(o_copies)
    loads["av"].wait()
    for k in range(n_out):
        loads["ow", k].wait()
    for copy in o_copies:
        copy.wait_recv()

    parts, maxima, totals = [], [], []
    for k in range(n_all):
        part = o_recv[k].astype(f32)
        parts.append(part[:, :rank])
        s = part[:, rank:]
        maxima.append(s[:, 0:1] + s[:, 1:2] + s[:, 2:3])
        totals.append(s[:, 3:4] + s[:, 4:5] + s[:, 5:6])
    top = functools.reduce(jnp.maximum, maxima)
    factors = [jnp.exp(m - top) for m in maxima]
    total_own = sum(f * t for f, t in zip(factors, totals))
    context_own = sum(f * p for f, p in zip(factors, parts))
    attended = (context_own / total_own).astype(bf16)
    head_values = jnp.dot(attended, av_buf[0], preferred_element_type=f32).astype(bf16)
    y_copies = []
    for k in range(1, n_out):
        y_send[k] = jnp.dot(head_values, ow_buf[k], preferred_element_type=f32).astype(y_send.dtype)
        to = (me_out + k) % n_out
        copy = remote(
            y_send.at[k], y_recv.at[k], y_ssem.at[k], y_rsem.at[k],
            (g, to // n_head, to % n_head, r),
        )
        copy.start()
        y_copies.append(copy)
    copies.extend(y_copies)
    result = jnp.dot(head_values, ow_buf[0], preferred_element_type=f32)
    for k in range(1, n_out):
        y_copies[k - 1].wait_recv()
        result = result + y_recv[k].astype(f32)
    out[...] = result.astype(out.dtype)
    for copy in copies:
        copy.wait_send()


def fused(mesh, hidden, kv_down, kv_gain, queries, absorb_key, absorb_value, out_weight, lengths):
    n_ctx, n_head, n_rep = (mesh.shape[a] for a in ("ctx", "head", "rep"))
    n_all, n_out = n_ctx * n_head * n_rep, n_ctx * n_head
    tok_rows, width_dev = hidden.shape
    rows = tok_rows // (n_head * n_rep)
    rank = kv_gain.shape[0]
    latent_width = kv_down.shape[1]
    rope = latent_width - rank
    conts = queries.shape[0]
    padded = rank + LANES
    out_cols = out_weight.shape[1] // n_out
    positions = -(-(n_ctx * tok_rows + 1) // 8) * 8
    table = jnp.asarray(rotary_table(positions, rope))
    f32, bf16 = jnp.float32, jnp.bfloat16
    dma = lambda *shape: pltpu.SemaphoreType.DMA(shape)
    any_space = pl.BlockSpec(memory_space=pl.ANY)
    vmem = pltpu.VMEM
    n_loads = n_head * n_rep + 6 + n_out
    pair_c, pair_r = (n_head, n_rep, rows, rank), (n_head, n_rep, rows // 2, 2 * rope)
    return pl.pallas_call(
        functools.partial(fused_kernel, n_ctx, n_head, n_rep),
        out_shape=jax.ShapeDtypeStruct((conts, out_cols), bf16),
        in_specs=[any_space] * 7 + [pl.BlockSpec(memory_space=pltpu.SMEM), any_space],
        out_specs=pl.BlockSpec(memory_space=vmem),
        scratch_shapes=[
            vmem((n_head, n_rep * rows, width_dev), bf16),
            vmem(kv_down.shape[::-1], bf16),
            vmem((1, rank), f32),
            vmem((1, conts, queries.shape[2]), bf16),
            vmem(absorb_key.shape, bf16),
            vmem(absorb_value.shape, bf16),
            vmem((n_out, out_weight.shape[0], out_cols), bf16),
            vmem(table.shape, f32),
            vmem(pair_c, f32), vmem(pair_r, f32),
            vmem(pair_c, f32), vmem(pair_r, f32),
            vmem(pair_c[:1] + pair_c[2:], f32), vmem(pair_r[:1] + pair_r[2:], f32),
            vmem(pair_c[:1] + pair_c[2:], f32), vmem(pair_r[:1] + pair_r[2:], f32),
            vmem((n_all, conts, padded), bf16),
            vmem((n_all, conts, padded), bf16),
            vmem((n_all, conts, padded), bf16),
            vmem((n_out, conts, out_cols), bf16),
            vmem((n_out, conts, out_cols), bf16),
            dma(n_loads),
            dma(n_head * n_rep * 2), dma(n_head * n_rep * 2),
            dma(n_head * 2), dma(n_head * 2),
            dma(n_all), dma(n_all), dma(n_all), dma(n_all), dma(n_out), dma(n_out),
        ],
        compiler_params=pltpu.CompilerParams(collective_id=0, has_side_effects=True),
    )(
        hidden, kv_down.T, kv_gain.reshape(1, rank), queries.swapaxes(0, 1), absorb_key, absorb_value,
        out_weight, lengths, table,
    )


def body(mesh, *arrays):
    hidden, kv_down, kv_gain, queries, absorb_key, _, out_weight, _ = arrays
    n_ctx, n_head, n_rep = (mesh.shape[a] for a in ("ctx", "head", "rep"))
    rope = kv_down.shape[1] - kv_gain.shape[0]
    whole_tiles = (
        queries.shape[1] == 1
        and 2 * rope == LANES
        and queries.shape[2] - absorb_key.shape[1] == rope
        and kv_gain.shape[0] % LANES == 0
        and hidden.shape[0] % (n_head * n_rep * 32) == 0
        and out_weight.shape[1] % (n_ctx * n_head * LANES) == 0
    )
    return fused(mesh, *arrays) if whole_tiles else shards(*arrays)


def solution(mesh):
    return jax.shard_map(
        functools.partial(body, mesh),
        mesh=mesh,
        in_specs=(
            P(("groups", "ctx"), ("head", "rep")),
            P(("head", "rep"), None),
            P(),
            P(("groups", "rep"), ("ctx", "head"), None),
            P(("ctx", "head"), None, None),
            P(("ctx", "head"), None, None),
            P(("ctx", "head"), None),
            P(("groups", "rep")),
        ),
        out_specs=P(("groups", "rep"), ("ctx", "head")),
        check_vma=False,
    )
```

```python
import functools

import jax
import jax.numpy as jnp
import numpy as np
from jax import lax
from jax.experimental import pallas as pl
from jax.experimental.pallas import tpu as pltpu
from jax.sharding import PartitionSpec as P

MESH = pl.DeviceIdType.MESH
LANES = 128
CHUNK = 256
STEP = 64


def rotate(vectors, position):
    half_width = vectors.shape[-1] // 2
    frequency = 10000.0 ** (-jnp.arange(half_width, dtype=jnp.float32) / half_width)
    angles = position.astype(jnp.float32)[..., None] * frequency
    first_half = vectors[..., :half_width]
    second_half = vectors[..., half_width:]
    return jnp.concatenate(
        [
            first_half * jnp.cos(angles) - second_half * jnp.sin(angles),
            first_half * jnp.sin(angles) + second_half * jnp.cos(angles),
        ],
        -1,
    )


def finish_rows(latent, kv_gain, first_row):
    rank_width = kv_gain.shape[0]
    compressed = latent[:, :rank_width]
    normed = (
        compressed
        * lax.rsqrt(jnp.mean(compressed * compressed, -1, keepdims=True) + 1e-06)
        * kv_gain
    )
    positions = first_row + jnp.arange(latent.shape[0], dtype=jnp.int32)
    return jnp.concatenate([normed, rotate(latent[:, rank_width:], positions)], -1).astype(
        jnp.bfloat16
    )


def shards(hidden, kv_down, kv_gain, queries, absorb_key, absorb_value, out_weight, lengths):
    tok_rows = hidden.shape[0]
    rank_width = kv_gain.shape[0]
    nope_width = absorb_key.shape[1]
    heads_dev = queries.shape[1]
    first_row = lax.axis_index("ctx") * tok_rows
    partial_value = jnp.dot(hidden, kv_down, preferred_element_type=jnp.float32)
    whole_latent = lax.psum(partial_value, ("head", "rep"))
    kv_cache = finish_rows(whole_latent, kv_gain, first_row)
    q_latent = jnp.einsum(
        "bhn,hnr->bhr", queries[..., :nope_width], absorb_key, preferred_element_type=jnp.float32
    )
    q_rotary = rotate(queries[..., nope_width:].astype(jnp.float32), lengths[:, None])
    softmax_scale = queries.shape[2] ** (-0.5)
    qcat = (jnp.concatenate([q_latent, q_rotary], -1) * softmax_scale).astype(jnp.bfloat16)
    gathered = lax.all_gather(qcat, "ctx", axis=1, tiled=True)
    cont_rows = gathered.shape[0]
    head_rows = gathered.shape[1]
    flat_queries = gathered.reshape(cont_rows * head_rows, gathered.shape[2])
    scores = jnp.dot(flat_queries, kv_cache.T, preferred_element_type=jnp.float32).reshape(
        cont_rows, head_rows, tok_rows
    )
    positions = first_row + jnp.arange(tok_rows, dtype=jnp.int32)
    visible = positions[None, None, :] < lengths[:, None, None]
    masked = jnp.where(visible, scores, -1e30)
    row_max = jnp.max(masked, -1)
    weights = jnp.where(visible, jnp.exp(masked - row_max[..., None]), 0.0)
    denominator = jnp.sum(weights, -1)
    flat_weights = weights.astype(jnp.bfloat16).reshape(cont_rows * head_rows, tok_rows)
    context = jnp.dot(
        flat_weights, kv_cache[:, :rank_width], preferred_element_type=jnp.float32
    ).reshape(cont_rows, head_rows, rank_width)
    top_peak = lax.pmax(row_max, "ctx")
    factor = jnp.exp(row_max - top_peak)
    total_own, context_own = (
        lax.psum_scatter(
            (denominator * factor).astype(jnp.bfloat16), "ctx", scatter_dimension=1, tiled=True
        ).astype(jnp.float32),
        lax.psum_scatter(
            (context * factor[..., None]).astype(jnp.bfloat16),
            "ctx",
            scatter_dimension=1,
            tiled=True,
        ).astype(jnp.float32),
    )
    attended = (context_own / total_own[..., None]).astype(jnp.bfloat16)
    head_values = jnp.einsum(
        "bhr,hrv->bhv", attended, absorb_value, preferred_element_type=jnp.float32
    ).astype(jnp.bfloat16)
    flat_values = head_values.reshape(cont_rows, heads_dev * head_values.shape[2])
    out_partial = jnp.dot(flat_values, out_weight, preferred_element_type=jnp.float32)
    return lax.psum_scatter(out_partial, ("ctx", "head"), scatter_dimension=1, tiled=True).astype(
        jnp.bfloat16
    )


def rotary_table(positions, rope_width):
    half_width = rope_width // 2
    frequency = (
        10000.0 ** (-np.arange(half_width, dtype=np.float32) / np.float32(half_width)).astype(np.float64)
    ).astype(np.float32)
    angles = (positions.astype(np.float32)[:, None] * frequency).astype(np.float64)
    cosine, sine = np.cos(angles), np.sin(angles)
    return np.concatenate([cosine, cosine, -sine, sine], -1).astype(np.float32)


def swap_halves(x):
    half = x.shape[-1] // 2
    return jnp.concatenate([x[:, half:], x[:, :half]], -1)


def split3(x):
    first = x.astype(jnp.bfloat16).astype(jnp.float32)
    second = (x - first).astype(jnp.bfloat16).astype(jnp.float32)
    return first, second, x - first - second


def flip(index, mask):
    bit = 1
    flipped = index
    while bit <= mask:
        if mask & bit:
            flipped = flipped + bit * (1 - 2 * ((index // bit) % 2))
        bit *= 2
    return flipped


def lane_tile(columns, rows):
    lane = lax.broadcasted_iota(jnp.int32, (rows, LANES), 1)
    tile = jnp.zeros((rows, LANES), jnp.float32)
    for i, column in enumerate(columns):
        tile = jnp.where(lane == i, column, tile)
    return tile


def fused_kernel(
    n_ctx, n_head, n_rep, n_coarse,
    hidden, kv_down, gain, queries, absorb_key, absorb_value, out_weight, lengths, table, steps,
    out,
    h_buf, kd_buf, gain_buf, q_buf, ak_buf, av_buf, ow_buf, tab_buf, steps_buf,
    pc, pr, rc, rr, sc, sr, xc, xr,
    q_all, o_send, o_recv, y_send, y_recv,
    load_sem, rep_send, rep_recv, head_send, head_recv,
    q_ssem, q_rsem, o_ssem, o_rsem, y_ssem, y_rsem, plane_go, all_go,
):
    g, c = lax.axis_index("groups"), lax.axis_index("ctx")
    h, r = lax.axis_index("head"), lax.axis_index("rep")
    n_all, n_out = n_ctx * n_head * n_rep, n_ctx * n_head
    me, me_out = (c * n_head + h) * n_rep + r, c * n_head + h
    tok_rows = hidden.shape[0]
    rows = tok_rows // (n_head * n_rep)
    rank = gain_buf.shape[1]
    conts = queries.shape[1]
    nope = absorb_key.shape[1]
    rope = queries.shape[2] - nope
    width = q_all.shape[2]
    out_cols = y_send.shape[2]
    f32, bf16 = jnp.float32, jnp.bfloat16
    base = c * tok_rows + (h * n_rep + r) * rows
    n_chunks = rank // CHUNK
    columns = [(j * CHUNK, CHUNK) for j in range(n_chunks)] + [(rank, rope)]
    n_parts = len(columns)

    def peer(index):
        return (g, index // (n_head * n_rep), (index // n_rep) % n_head, index % n_rep)

    def signal(semaphore, device):
        pl.semaphore_signal(semaphore, inc=1, device_id=device, device_id_type=MESH)

    n_plane = n_head * n_rep
    member = h * n_rep + r
    barrier = pltpu.get_barrier_semaphore()

    @pl.when(member != 0)
    def _():
        signal(barrier, (g, c, 0, 0))

    loads = {}

    def load(name, source, target):
        loads[name] = pltpu.make_async_copy(source, target, load_sem.at[len(loads)])
        loads[name].start()

    head_order = list(range(1, n_head)) + [0]

    def load_hidden(k):
        for k2 in range(n_rep):
            block = flip(h, k) * n_rep + flip(r, k2)
            load(
                ("hidden", k, k2),
                hidden.at[pl.ds(pl.multiple_of(block * rows, 8), rows), :],
                h_buf.at[k, pl.ds(k2 * rows, rows), :],
            )

    load("q", queries, q_buf)
    load("ak", absorb_key, ak_buf)
    load("steps", steps, steps_buf)
    load_hidden(head_order[0])
    for j, (start, size) in enumerate(columns):
        load(("kd", j), kv_down.at[pl.ds(start, size), :], kd_buf.at[pl.ds(start, size), :])

    def load_rest():
        for k in head_order[1:]:
            load_hidden(k)
        load("gain", gain, gain_buf)
        load("table", table.at[pl.ds(pl.multiple_of(base, 8), rows), :], tab_buf)
        load("av", absorb_value, av_buf)
        for k in range(n_out):
            out_start = pl.multiple_of(flip(me_out, k) * out_cols, LANES)
            load(("ow", k), out_weight.at[:, pl.ds(out_start, out_cols)], ow_buf.at[k])

    @pl.when(member == 0)
    def _():
        pl.semaphore_wait(barrier, n_plane - 1)
        for k in range(1, n_plane):
            signal(plane_go, (g, c, k // n_rep, k % n_rep))

    @pl.when(member != 0)
    def _():
        pl.semaphore_wait(plane_go, 1)

    @pl.when(member == 1)
    def _():
        for k in range(1, n_ctx):
            signal(barrier, (g, flip(c, k), h, r))

    def remote(source, target, send_sem, recv_sem, device):
        return pltpu.make_async_remote_copy(
            src_ref=source, dst_ref=target, send_sem=send_sem, recv_sem=recv_sem,
            device_id=device, device_id_type=MESH,
        )

    copies = []

    def part_of(compressed, rotary, index, j):
        return compressed.at[index + (j,)] if j < n_chunks else rotary.at[index]

    def project(k, j):
        start, size = columns[j]
        block = lax.dot_general(
            h_buf[k], kd_buf[start : start + size, :], (((1,), (1,)), ((), ())),
            preferred_element_type=f32,
        )
        for k2 in range(n_rep):
            own = block[k2 * rows : (k2 + 1) * rows]
            if j < n_chunks:
                pc[k, k2, j] = own
            else:
                pr[k, k2] = jnp.concatenate([own[: rows // 2], own[rows // 2 :]], -1)
        started = []
        for k2 in range(1, n_rep):
            slot = (k * n_rep + k2) * n_parts + j
            copy = remote(
                part_of(pc, pr, (k, k2), j), part_of(rc, rr, (k, k2), j),
                rep_send.at[slot], rep_recv.at[slot], (g, c, h, flip(r, k2)),
            )
            copy.start()
            started.append(copy)
        copies.extend(started)
        return started

    def sum_rep(k, j, started):
        for copy in started:
            copy.wait_recv()
        total = part_of(pc, pr, (k, 0), j)[...]
        for k2 in range(1, n_rep):
            total = total + part_of(rc, rr, (k, k2), j)[...]
        part_of(sc, sr, (k,), j)[...] = total

    def exchange_head(k, j):
        slot = k * n_parts + j
        copy = remote(
            part_of(sc, sr, (k,), j), part_of(xc, xr, (k,), j),
            head_send.at[slot], head_recv.at[slot], (g, c, flip(h, k), r),
        )
        copy.start()
        copies.append(copy)
        sent.append(copy)

    for name in ("q", "ak", "steps"):
        loads[name].wait()
    own_q = q_buf[0]
    q_latent = jnp.dot(own_q[:, :nope], ak_buf[0], preferred_element_type=f32)
    q_rotary = own_q[:, nope:].astype(f32)
    coarse, fine = (
        jnp.concatenate([steps_buf[pl.ds(row, 1), :] for row in index], 0)
        for index in (
            [lengths[b] // STEP for b in range(conts)],
            [n_coarse + lengths[b] % STEP for b in range(conts)],
        )
    )
    cosine = coarse[:, :rope] * fine[:, :rope] - coarse[:, rope:] * fine[:, rope:]
    sine = coarse[:, rope:] * fine[:, :rope] + coarse[:, :rope] * fine[:, rope:]
    q_rotary = q_rotary * cosine + swap_halves(q_rotary) * sine
    scale = queries.shape[2] ** (-0.5)
    row = lax.broadcasted_iota(jnp.int32, (conts, LANES), 0)
    length_rows = jnp.zeros((conts, LANES), jnp.int32)
    for b in range(conts):
        length_rows = jnp.where(row == b, lengths[b], length_rows)
    high = length_rows // STEP
    lane = lax.broadcasted_iota(jnp.int32, (conts, LANES), 1)
    extra = jnp.where(lane == 0, high, length_rows - high * STEP).astype(f32)[:, : width - rank - rope]
    qcat = jnp.concatenate([q_latent * scale, q_rotary * scale, extra], -1)
    q_all[0] = qcat.astype(bf16)
    q_copies = []
    for k in range(1, n_plane):
        copy = remote(q_all.at[0], q_all.at[k], q_ssem.at[k], q_rsem.at[k], peer(flip(me, k)))
        copy.start()
        q_copies.append(copy)
    copies.extend(q_copies)

    load_rest()
    sent = []
    pending = []

    def drain():
        k, j, started = pending.pop(0)
        sum_rep(k, j, started)
        if k:
            exchange_head(k, j)

    for k in head_order[:-1]:
        for k2 in range(n_rep):
            loads["hidden", k, k2].wait()
        for j in range(n_parts):
            if k == head_order[0]:
                loads["kd", j].wait()
            pending.append((k, j, project(k, j)))
            if len(pending) > 1:
                drain()
    while pending:
        drain()
    for k2 in range(n_rep):
        loads["hidden", 0, k2].wait()
    for j in range(n_parts):
        pending.append((0, j, project(0, j)))

    for copy in q_copies:
        copy.wait_recv()

    @pl.when(member == 1)
    def _():
        pl.semaphore_wait(barrier, n_ctx - 1)
        for k in range(n_plane):
            if k != 1:
                signal(all_go, (g, c, k // n_rep, k % n_rep))

    @pl.when(member != 1)
    def _():
        pl.semaphore_wait(all_go, 1)

    q_far = []
    for k in range(n_ctx - 1, 0, -1):
        copy = remote(
            q_all.at[pl.ds(0, n_plane)], q_all.at[pl.ds(k * n_plane, n_plane)],
            q_ssem.at[n_plane + k], q_rsem.at[n_plane + k], (g, flip(c, k), h, r),
        )
        copy.start()
        q_far.append(copy)
    copies.extend(q_far)

    while pending:
        drain()
    for copy in q_far:
        copy.wait_recv()
    q_rows = jnp.concatenate([q_all[k].astype(f32) for k in range(n_all)], 0)
    q_lengths = q_rows[:, rank + rope : rank + rope + 1] * float(STEP) + q_rows[
        :, rank + rope + 1 : rank + rope + 2
    ]
    loads["gain"].wait()
    loads["table"].wait()
    token_table = tab_buf[...]

    for copy in sent:
        copy.wait_recv()
    latent_c, latent_r = [sc[0, j] for j in range(n_chunks)], sr[0]
    for k in range(1, n_head):
        latent_c = [latent_c[j] + xc[k, j] for j in range(n_chunks)]
        latent_r = latent_r + xr[k]
    latent_c = jnp.concatenate(latent_c, -1)
    latent_r = jnp.concatenate([latent_r[:, :rope], latent_r[:, rope:]], 0)
    normed = (
        latent_c
        * lax.rsqrt(jnp.mean(latent_c * latent_c, -1, keepdims=True) + 1e-06)
        * gain_buf[...]
    )
    rotary = latent_r * token_table[:, :rope] + swap_halves(latent_r) * token_table[:, rope:]
    kv_c = normed.astype(bf16)
    kv = jnp.concatenate(
        [normed, rotary, jnp.zeros((rows, width - rank - rope), f32)], -1
    ).astype(bf16)
    scores = lax.dot_general(
        q_rows.astype(bf16), kv, (((1,), (1,)), ((), ())), preferred_element_type=f32
    )
    n_q = n_all * conts
    positions = (base + lax.broadcasted_iota(jnp.int32, (n_q, rows), 1)).astype(f32)
    visible = positions < q_lengths
    masked = jnp.where(visible, scores, -1e30)
    row_max = jnp.max(masked, -1, keepdims=True)
    weights = jnp.where(visible, jnp.exp(masked - row_max), 0.0)
    total = jnp.sum(weights, -1, keepdims=True)
    context = jnp.dot(weights.astype(bf16), kv_c, preferred_element_type=f32)
    stats = lane_tile(split3(row_max) + split3(total), n_q)
    for k in range(n_all):
        block = slice(k * conts, (k + 1) * conts)
        target = o_recv if k == 0 else o_send
        target[k, :, :rank] = context[block].astype(bf16)
        target[k, :, rank:] = stats[block].astype(bf16)
    o_copies = []
    for k in range(n_all - 1, 0, -1):
        copy = remote(
            o_send.at[k], o_recv.at[k], o_ssem.at[k], o_rsem.at[k], peer(flip(me, k))
        )
        copy.start()
        o_copies.append(copy)
    copies.extend(o_copies)
    loads["av"].wait()
    for k in range(n_out):
        loads["ow", k].wait()
    for copy in o_copies:
        copy.wait_recv()

    parts, maxima, totals = [], [], []
    for k in range(n_all):
        part = o_recv[k].astype(f32)
        parts.append(part[:, :rank])
        s = part[:, rank:]
        maxima.append(s[:, 0:1] + s[:, 1:2] + s[:, 2:3])
        totals.append(s[:, 3:4] + s[:, 4:5] + s[:, 5:6])
    top = functools.reduce(jnp.maximum, maxima)
    factors = [jnp.exp(m - top) for m in maxima]
    total_own = sum(f * t for f, t in zip(factors, totals))
    context_own = sum(f * p for f, p in zip(factors, parts))
    attended = (context_own / total_own).astype(bf16)
    head_values = jnp.dot(attended, av_buf[0], preferred_element_type=f32).astype(bf16)
    y_copies = []
    for k in range(n_out - 1, 0, -1):
        y_send[k] = jnp.dot(head_values, ow_buf[k], preferred_element_type=f32).astype(y_send.dtype)
        to = flip(me_out, k)
        copy = remote(
            y_send.at[k], y_recv.at[k], y_ssem.at[k], y_rsem.at[k],
            (g, to // n_head, to % n_head, r),
        )
        copy.start()
        y_copies.append(copy)
    copies.extend(y_copies)
    result = jnp.dot(head_values, ow_buf[0], preferred_element_type=f32)
    for k in range(1, n_out):
        y_copies[n_out - 1 - k].wait_recv()
        result = result + y_recv[k].astype(f32)
    out[...] = result.astype(out.dtype)
    for copy in copies:
        copy.wait_send()


def fused(mesh, hidden, kv_down, kv_gain, queries, absorb_key, absorb_value, out_weight, lengths):
    n_ctx, n_head, n_rep = (mesh.shape[a] for a in ("ctx", "head", "rep"))
    n_all, n_out = n_ctx * n_head * n_rep, n_ctx * n_head
    tok_rows, width_dev = hidden.shape
    rows = tok_rows // (n_head * n_rep)
    rank = kv_gain.shape[0]
    latent_width = kv_down.shape[1]
    rope = latent_width - rank
    conts = queries.shape[0]
    padded = rank + LANES
    out_cols = out_weight.shape[1] // n_out
    tokens = n_ctx * tok_rows
    table = jnp.asarray(rotary_table(np.arange(tokens), rope))
    n_coarse = tokens // STEP + 1
    step_positions = np.concatenate([np.arange(n_coarse) * STEP, np.arange(STEP)])
    step_positions = np.pad(step_positions, (0, -len(step_positions) % 8))
    steps = jnp.asarray(rotary_table(step_positions, rope))
    f32, bf16 = jnp.float32, jnp.bfloat16
    dma = lambda *shape: pltpu.SemaphoreType.DMA(shape)
    any_space = pl.BlockSpec(memory_space=pl.ANY)
    vmem = pltpu.VMEM
    n_parts = rank // CHUNK + 1
    n_loads = n_head * n_rep + n_parts + 6 + n_out
    pair_c = (n_head, n_rep, rank // CHUNK, rows, CHUNK)
    pair_r = (n_head, n_rep, rows // 2, 2 * rope)
    return pl.pallas_call(
        functools.partial(fused_kernel, n_ctx, n_head, n_rep, n_coarse),
        out_shape=jax.ShapeDtypeStruct((conts, out_cols), bf16),
        in_specs=[any_space] * 7 + [pl.BlockSpec(memory_space=pltpu.SMEM), any_space, any_space],
        out_specs=pl.BlockSpec(memory_space=vmem),
        scratch_shapes=[
            vmem((n_head, n_rep * rows, width_dev), bf16),
            vmem(kv_down.shape[::-1], bf16),
            vmem((1, rank), f32),
            vmem((1, conts, queries.shape[2]), bf16),
            vmem(absorb_key.shape, bf16),
            vmem(absorb_value.shape, bf16),
            vmem((n_out, out_weight.shape[0], out_cols), bf16),
            vmem((rows, 2 * rope), f32),
            vmem(steps.shape, f32),
            vmem(pair_c, f32), vmem(pair_r, f32),
            vmem(pair_c, f32), vmem(pair_r, f32),
            vmem(pair_c[:1] + pair_c[2:], f32), vmem(pair_r[:1] + pair_r[2:], f32),
            vmem(pair_c[:1] + pair_c[2:], f32), vmem(pair_r[:1] + pair_r[2:], f32),
            vmem((n_all, conts, padded), bf16),
            vmem((n_all, conts, padded), bf16),
            vmem((n_all, conts, padded), bf16),
            vmem((n_out, conts, out_cols), bf16),
            vmem((n_out, conts, out_cols), bf16),
            dma(n_loads),
            dma(n_head * n_rep * n_parts), dma(n_head * n_rep * n_parts),
            dma(n_head * n_parts), dma(n_head * n_parts),
            dma(n_head * n_rep + n_ctx), dma(n_head * n_rep + n_ctx),
            dma(n_all), dma(n_all), dma(n_out), dma(n_out),
            pltpu.SemaphoreType.REGULAR, pltpu.SemaphoreType.REGULAR,
        ],
        compiler_params=pltpu.CompilerParams(collective_id=0, has_side_effects=True),
    )(
        hidden, kv_down.T, kv_gain.reshape(1, rank), queries.swapaxes(0, 1), absorb_key, absorb_value,
        out_weight, lengths, table, steps,
    )


def body(mesh, *arrays):
    hidden, kv_down, kv_gain, queries, absorb_key, _, out_weight, _ = arrays
    n_ctx, n_head, n_rep = (mesh.shape[a] for a in ("ctx", "head", "rep"))
    rope = kv_down.shape[1] - kv_gain.shape[0]
    sizes = (n_ctx, n_head, n_rep)
    whole_tiles = (
        all(n > 1 and n & (n - 1) == 0 for n in sizes)
        and queries.shape[1] == 1
        and 2 * rope == LANES
        and queries.shape[2] - absorb_key.shape[1] == rope
        and kv_gain.shape[0] % CHUNK == 0
        and hidden.shape[0] % (n_head * n_rep * 32) == 0
        and out_weight.shape[1] % (n_ctx * n_head * LANES) == 0
    )
    return fused(mesh, *arrays) if whole_tiles else shards(*arrays)


def solution(mesh):
    return jax.shard_map(
        functools.partial(body, mesh),
        mesh=mesh,
        in_specs=(
            P(("groups", "ctx"), ("head", "rep")),
            P(("head", "rep"), None),
            P(),
            P(("groups", "rep"), ("ctx", "head"), None),
            P(("ctx", "head"), None, None),
            P(("ctx", "head"), None, None),
            P(("ctx", "head"), None),
            P(("groups", "rep")),
        ),
        out_specs=P(("groups", "rep"), ("ctx", "head")),
        check_vma=False,
    )
```
